32 devices in a mesh: seqb: 4 (over x, core), seqt: 2 (over y), ch: 4 (over z).
Axes of the slice: x: 2, y: 2, z: 4, core: 2. Of those that a mesh axis runs over, the one named last changes fastest.
Arguments:
- query_gate: bfloat16 [2048, 4096], P(('seqb', 'seqt'), 'ch'), may hold values from -6 to 6
- key_proj: bfloat16 [2048, 4096], P(('seqb', 'seqt'), 'ch'), may hold values from -6 to 6
- value_proj: bfloat16 [2048, 4096], P(('seqb', 'seqt'), 'ch'), may hold values from -6 to 6
- filters: float32 [2048, 4096], P(('seqb', 'seqt'), 'ch'), may hold values from -4 to 4
- skip_gain: float32 [4096], P('ch'), may hold values from 0.5 to 2
- w_out: bfloat16 [4096, 4096], P('ch', ('seqb', 'seqt')), may hold values from -0.09375 to 0.09375
Outputs:
- layer_out: bfloat16 [2048, 4096], P(('seqb', 'seqt'), 'ch')
The draws below stay inside these ranges and needn't reach their ends.
All inputs are finite; a program needn't handle non-finite values.
Results may differ from the reference program's by a relative error of at most 0.0049.
Values may be sent and summed in bfloat16 or wider, within the bound.
A program may use at most 128 MiB of HBM per device.

```python
import math
import jax
import jax.numpy as jnp
from jax import lax

D = 4096
TOKENS = 2048


def draw_filters(key, part):
    base = jax.random.fold_in(key, 31)
    rate_key, value_key = jax.random.split(base)
    position = jnp.arange(TOKENS, dtype=jnp.float32)[:, None]
    log_rate = jax.random.uniform(rate_key, (1, D), jnp.float32, math.log(0.3 / TOKENS), math.log(1.0 / 30.0))
    values = jnp.clip(jax.random.normal(value_key, (TOKENS, D), jnp.float32), -4.0, 4.0)
    rate = jnp.exp(log_rate)
    return values * jnp.exp(-rate * position) * jnp.sqrt(1.0 - jnp.exp(-2.0 * rate))


def level_of(rng, dims, cuts, least, largest):
    def one(dim, shards_of):
        steps = jax.random.uniform(jax.random.fold_in(jax.random.fold_in(rng, 6), dim), (shards_of,), jnp.float32, least / len(cuts), largest / len(cuts))
        return jnp.repeat(jnp.exp(steps), dims[dim] // shards_of).reshape((-1,) + (1,) * (len(dims) - dim - 1))

    factor_of = one(*cuts[0])
    for cut in cuts[1:]:
        factor_of = factor_of * one(*cut)
    return factor_of


def scatter_about(own_key, extent, spread, bound, cuts=(), kind=jnp.bfloat16):
    entries = spread * jax.random.normal(own_key, extent, jnp.float32)
    if cuts:
        entries = entries * level_of(own_key, extent, cuts, -0.22, 0.18)
    return jnp.clip(entries, -bound, bound).astype(kind)


def setup_inputs(seed: int = 0) -> dict:
    seeds = jax.random.split(jax.random.key(seed), 7)
    query_gate = scatter_about(seeds[0], (TOKENS, D), 1.0, 6.0, ((0, 8), (1, 4)))
    key_proj = scatter_about(seeds[1], (TOKENS, D), 1.0, 6.0, ((0, 8), (1, 4)))
    value_proj = scatter_about(seeds[2], (TOKENS, D), 1.0, 6.0, ((0, 8), (1, 4)))
    filters = draw_filters(jax.random.fold_in(seeds[6], 71), 0)
    skip_gain = jnp.clip(0.5 + 1.5 * jax.random.uniform(seeds[4], (D,), jnp.float32) ** level_of(seeds[4], (D,), ((0, 4),), -0.2, 0.2), 0.5, 2.0)
    w_out = scatter_about(seeds[5], (D, D), D ** -0.5, 0.09375, ((0, 4), (1, 8)))
    return dict(query_gate=query_gate, key_proj=key_proj, value_proj=value_proj, filters=filters, skip_gain=skip_gain, w_out=w_out)


def reference(query_gate, key_proj, value_proj, filters, skip_gain, w_out):
    product = key_proj.astype(jnp.float32) * value_proj.astype(jnp.float32)
    block_width = min(D, 256)
    block_count = D // block_width

    def convolve_block(block_pair):
        signal_block, filter_block = block_pair
        spectrum = jnp.fft.rfft(signal_block, n=2 * TOKENS, axis=0)
        response = jnp.fft.rfft(filter_block, n=2 * TOKENS, axis=0)
        return jnp.fft.irfft(spectrum * response, n=2 * TOKENS, axis=0)[:TOKENS].astype(jnp.float32)

    signal_blocks = product.reshape(TOKENS, block_count, block_width).transpose(1, 0, 2)
    filter_blocks = filters.astype(jnp.float32).reshape(TOKENS, block_count, block_width).transpose(1, 0, 2)
    convolved = lax.map(convolve_block, (signal_blocks, filter_blocks))
    convolved = convolved.transpose(1, 0, 2).reshape(TOKENS, D)
    gated_rows = (query_gate.astype(jnp.float32) * (convolved + skip_gain[None, :] * product)).astype(jnp.bfloat16)
    return jnp.dot(gated_rows, w_out, preferred_element_type=jnp.float32).astype(jnp.bfloat16)
```

```python
import numpy as np

import jax
import jax.numpy as jnp
from jax import lax
from jax.experimental import pallas as pl
from jax.experimental.pallas import tpu as pltpu
from jax.sharding import PartitionSpec as P

SEQ = ("seqb", "seqt")


def split(x):
    hi = x.astype(jnp.bfloat16)
    return hi, (x - hi.astype(jnp.float32)).astype(jnp.bfloat16)


def dot32(m_hi, m_lo, a):
    a_hi, a_lo = split(a)
    dot = lambda p, q: jnp.dot(p, q, preferred_element_type=jnp.float32)
    return dot(m_hi, a_hi) + dot(m_lo, a_hi) + dot(m_hi, a_lo)


def conv_kernel(coef_ref, x_ref, base_ref, twid_ref, out_ref, acc_ref):
    blocks, rows, both = x_ref.shape
    width = both // 2
    k = pl.program_id(0)

    @pl.when(k == 0)
    def _():
        acc_ref[...] = jnp.zeros_like(acc_ref)

    re = jnp.zeros((rows, both), jnp.float32)
    im = jnp.zeros((rows, both), jnp.float32)
    for n in range(blocks):
        x = x_ref[n].astype(jnp.float32)
        re += coef_ref[0, k, n] * x
        im -= coef_ref[1, k, n] * x
    tc = twid_ref[0, :, 0:1]
    ts = twid_ref[0, :, 1:2]
    a = jnp.concatenate([re * tc + im * ts, im * tc - re * ts], axis=1)
    p = dot32(base_ref[0], base_ref[1], a)
    q = dot32(base_ref[2], base_ref[3], a)
    br = p[:, :both] + q[:, both:]
    bi = p[:, both:] - q[:, :both]
    sr, fr = br[:, :width], br[:, width:]
    si, fi = bi[:, :width], bi[:, width:]
    y = jnp.concatenate([sr * fr - si * fi, sr * fi + si * fr], axis=1)
    p = dot32(base_ref[0], base_ref[1], y)
    q = dot32(base_ref[2], base_ref[3], y)
    zr = p[:, :width] - q[:, width:]
    zi = p[:, width:] + q[:, :width]
    vr = zr * tc - zi * ts
    vi = zi * tc + zr * ts
    for n in range(blocks):
        acc_ref[n] += coef_ref[2, k, n] * vr - coef_ref[3, k, n] * vi

    @pl.when(k == blocks)
    def _():
        out_ref[...] = acc_ref[...].astype(out_ref.dtype)


def tables(blocks, rows):
    period = 2 * blocks * rows
    k = np.arange(blocks + 1)
    n = np.arange(blocks)
    ang = 2 * np.pi * ((k[:, None] * n[None, :]) % (2 * blocks)) / (2 * blocks)
    gain = np.where((k == 0) | (k == blocks), 1.0, 2.0)[:, None] / period
    coef = np.stack([np.cos(ang), np.sin(ang), gain * np.cos(ang), gain * np.sin(ang)])
    r = np.arange(rows)
    ang = 2 * np.pi * ((r[:, None] * r[None, :]) % rows) / rows
    parts = []
    for m in (np.cos(ang), np.sin(ang)):
        hi = m.astype(jnp.bfloat16)
        parts += [hi, (m - hi.astype(np.float64)).astype(jnp.bfloat16)]
    ang = 2 * np.pi * ((k[:, None] * r[None, :]) % period) / period
    twid = np.stack([np.cos(ang), np.sin(ang)], axis=-1)
    return coef.astype(np.float32), np.stack(parts), twid.astype(np.float32)


def convolve(columns):
    blocks, rows, both = columns.shape
    coef, base, twid = tables(blocks, rows)
    return pl.pallas_call(
        conv_kernel,
        grid=(blocks + 1,),
        out_shape=jax.ShapeDtypeStruct((blocks, rows, both // 2), jnp.bfloat16),
        in_specs=[
            pl.BlockSpec(memory_space=pltpu.SMEM),
            pl.BlockSpec((blocks, rows, both), lambda k: (0, 0, 0)),
            pl.BlockSpec((4, rows, rows), lambda k: (0, 0, 0)),
            pl.BlockSpec((1, rows, 2), lambda k: (k, 0, 0)),
        ],
        out_specs=pl.BlockSpec((blocks, rows, both // 2), lambda k: (0, 0, 0)),
        scratch_shapes=[pltpu.VMEM((blocks, rows, both // 2), jnp.float32)],
        compiler_params=pltpu.CompilerParams(vmem_limit_bytes=48 * 1024 * 1024),
        cost_estimate=pl.CostEstimate(
            flops=36 * (blocks + 1) * rows * rows * both, bytes_accessed=4 * 1024 * 1024, transcendentals=0
        ),
    )(jnp.asarray(coef), columns, jnp.asarray(base), jnp.asarray(twid))


def shards(query_gate, key_proj, value_proj, filters, skip_gain, w_out):
    rows, channels = key_proj.shape
    seq = lax.axis_size(SEQ)
    width = channels // seq
    product = key_proj.astype(jnp.float32) * value_proj.astype(jnp.float32)
    pieces = lambda a: a.astype(jnp.bfloat16).reshape(rows, seq, width).transpose(1, 0, 2)
    stacked = jnp.concatenate([pieces(product), pieces(filters)], axis=2)
    columns = lax.all_to_all(stacked, SEQ, split_axis=0, concat_axis=0, tiled=True)
    spatial = lax.all_to_all(convolve(columns), SEQ, split_axis=0, concat_axis=0, tiled=True)
    convolved = spatial.transpose(1, 0, 2).reshape(rows, channels).astype(jnp.float32)
    gated_rows = (
        query_gate.astype(jnp.float32) * (convolved + skip_gain[None, :] * product)
    ).astype(jnp.bfloat16)
    weights = lax.all_gather(w_out, SEQ, axis=1, tiled=True)
    partial_sums = jnp.dot(gated_rows, weights, preferred_element_type=jnp.float32)
    return lax.psum_scatter(partial_sums, "ch", scatter_dimension=1, tiled=True).astype(
        jnp.bfloat16
    )


def solution(mesh):
    return jax.shard_map(
        shards,
        mesh=mesh,
        in_specs=(
            P(SEQ, "ch"),
            P(SEQ, "ch"),
            P(SEQ, "ch"),
            P(SEQ, "ch"),
            P("ch"),
            P("ch", SEQ),
        ),
        out_specs=P(SEQ, "ch"),
        check_vma=False,
    )
```

```python
import numpy as np

import jax
import jax.numpy as jnp
from jax import lax
from jax.experimental import pallas as pl
from jax.experimental.pallas import tpu as pltpu
from jax.sharding import PartitionSpec as P

SEQ = ("seqb", "seqt")


def split(x):
    hi = x.astype(jnp.bfloat16)
    return hi, (x - hi.astype(jnp.float32)).astype(jnp.bfloat16)


def dot32(m_hi, m_lo, a):
    a_hi, a_lo = split(a)
    dot = lambda p, q: jnp.dot(p, q, preferred_element_type=jnp.float32)
    return dot(m_hi, a_hi) + dot(m_lo, a_hi) + dot(m_hi, a_lo)


def conv_kernel(coef_ref, x_ref, base_ref, twid_ref, out_ref, acc_ref):
    blocks, rows, both = x_ref.shape
    width = both // 2
    k = pl.program_id(0)

    @pl.when(k == 0)
    def _():
        acc_ref[...] = jnp.zeros_like(acc_ref)

    re = jnp.zeros((rows, both), jnp.float32)
    im = jnp.zeros((rows, both), jnp.float32)
    for n in range(blocks):
        x = x_ref[n].astype(jnp.float32)
        re += coef_ref[0, k, n] * x
        im -= coef_ref[1, k, n] * x
    tc = twid_ref[0, :, 0:1]
    ts = twid_ref[0, :, 1:2]
    a = jnp.concatenate([re * tc + im * ts, im * tc - re * ts], axis=1)
    p = dot32(base_ref[0], base_ref[1], a)
    q = dot32(base_ref[2], base_ref[3], a)
    br = p[:, :both] + q[:, both:]
    bi = p[:, both:] - q[:, :both]
    sr, fr = br[:, :width], br[:, width:]
    si, fi = bi[:, :width], bi[:, width:]
    y = jnp.concatenate([sr * fr - si * fi, sr * fi + si * fr], axis=1)
    p = dot32(base_ref[0], base_ref[1], y)
    q = dot32(base_ref[2], base_ref[3], y)
    zr = p[:, :width] - q[:, width:]
    zi = p[:, width:] + q[:, :width]
    vr = zr * tc - zi * ts
    vi = zi * tc + zr * ts
    for n in range(blocks):
        acc_ref[n] += coef_ref[2, k, n] * vr - coef_ref[3, k, n] * vi

    @pl.when(k == blocks)
    def _():
        out_ref[...] = acc_ref[...].astype(out_ref.dtype)


def tables(blocks, rows):
    period = 2 * blocks * rows
    k = np.arange(blocks + 1)
    n = np.arange(blocks)
    ang = 2 * np.pi * ((k[:, None] * n[None, :]) % (2 * blocks)) / (2 * blocks)
    gain = np.where((k == 0) | (k == blocks), 1.0, 2.0)[:, None] / period
    coef = np.stack([np.cos(ang), np.sin(ang), gain * np.cos(ang), gain * np.sin(ang)])
    r = np.arange(rows)
    ang = 2 * np.pi * ((r[:, None] * r[None, :]) % rows) / rows
    parts = []
    for m in (np.cos(ang), np.sin(ang)):
        hi = m.astype(jnp.bfloat16)
        parts += [hi, (m - hi.astype(np.float64)).astype(jnp.bfloat16)]
    ang = 2 * np.pi * ((k[:, None] * r[None, :]) % period) / period
    twid = np.stack([np.cos(ang), np.sin(ang)], axis=-1)
    return coef.astype(np.float32), np.stack(parts), twid.astype(np.float32)


def convolve(columns):
    blocks, rows, both = columns.shape
    coef, base, twid = tables(blocks, rows)
    return pl.pallas_call(
        conv_kernel,
        grid=(blocks + 1,),
        out_shape=jax.ShapeDtypeStruct((blocks, rows, both // 2), jnp.bfloat16),
        in_specs=[
            pl.BlockSpec(memory_space=pltpu.SMEM),
            pl.BlockSpec((blocks, rows, both), lambda k: (0, 0, 0)),
            pl.BlockSpec((4, rows, rows), lambda k: (0, 0, 0)),
            pl.BlockSpec((1, rows, 2), lambda k: (k, 0, 0)),
        ],
        out_specs=pl.BlockSpec((blocks, rows, both // 2), lambda k: (0, 0, 0)),
        scratch_shapes=[pltpu.VMEM((blocks, rows, both // 2), jnp.float32)],
        compiler_params=pltpu.CompilerParams(vmem_limit_bytes=48 * 1024 * 1024),
        cost_estimate=pl.CostEstimate(
            flops=36 * (blocks + 1) * rows * rows * both, bytes_accessed=4 * 1024 * 1024, transcendentals=0
        ),
    )(jnp.asarray(coef), columns, jnp.asarray(base), jnp.asarray(twid))


MESH = pl.DeviceIdType.MESH


def layer_kernel(coef_ref, q_ref, k_ref, v_ref, f_ref, skip_ref, w_ref, base_ref, twid_ref, out_ref,
                 xs_send, xs_recv, acc_ref, cs_send, cs_recv, g_ref, w_all, p_send, p_recv, p_own,
                 o_send, o_recv, in_s, in_r, back_s, back_r, w_s, w_r, g_s, g_r, p_s, p_r, o_s, o_r, local_sem):
    seq_t = lax.axis_size("seqt")
    blocks = lax.axis_size("seqb") * seq_t
    depth = lax.axis_size("ch")
    ib, it, z = lax.axis_index("seqb"), lax.axis_index("seqt"), lax.axis_index("ch")
    me = ib * seq_t + it
    core = ib % 2
    rows, channels = k_ref.shape
    width = channels // blocks
    both = 2 * width
    cols = w_ref.shape[1]
    per = blocks // depth
    place = lambda s: {"seqb": s // seq_t, "seqt": s % seq_t}
    sibling = {"seqb": ib + 1 - 2 * core}

    def remote(src, dst, send, recv, where):
        return pltpu.make_async_remote_copy(
            src_ref=src, dst_ref=dst, send_sem=send, recv_sem=recv, device_id=where, device_id_type=MESH
        )

    barrier = pltpu.get_barrier_semaphore()
    for j in range(1, blocks):
        pl.semaphore_signal(barrier, inc=1, device_id=place((me + j) % blocks), device_id_type=MESH)
    for j in range(1, depth):
        pl.semaphore_signal(barrier, inc=1, device_id={"ch": (z + j) % depth}, device_id_type=MESH)

    def piece(d):
        lanes = pl.ds(pl.multiple_of(d * width, width), width)
        p = k_ref[:, lanes].astype(jnp.float32) * v_ref[:, lanes].astype(jnp.float32)
        return jnp.concatenate([p.astype(jnp.bfloat16), f_ref[:, lanes].astype(jnp.bfloat16)], axis=1)

    for j in range(1, blocks):
        xs_send[j] = piece((me + j) % blocks)
    pl.semaphore_wait(barrier, blocks + depth - 2)

    entry = [
        remote(xs_send.at[j], xs_recv.at[me], in_s.at[j], in_r.at[j], place((me + j) % blocks))
        for j in range(1, blocks)
    ]
    for copy in entry:
        copy.start()
    xs_recv[me] = piece(me)

    keep = me % per
    targets = [
        ((x * 2 + keep) * seq_t + t, x * seq_t + t)
        for x in range(blocks // seq_t // 2)
        for t in range(seq_t)
    ]
    weight = [
        (dest, remote(w_ref, w_all.at[me // per], w_s.at[i], w_r.at[me // per], place(dest)))
        for dest, i in targets
    ]
    local = pltpu.make_async_copy(w_ref, w_all.at[me // per], local_sem)
    mine = core == keep

    @pl.when(mine)
    def _():
        local.start()

    def start_weights():
        for dest, copy in weight:
            @pl.when(dest != me)
            def _():
                copy.start()

    for copy in entry:
        copy.wait_recv()
    start_weights()

    acc_ref[...] = jnp.zeros_like(acc_ref)

    def frequency(k, carry):
        re = jnp.zeros((rows, both), jnp.float32)
        im = jnp.zeros((rows, both), jnp.float32)
        for n in range(blocks):
            x = xs_recv[n].astype(jnp.float32)
            re += coef_ref[0, k, n] * x
            im -= coef_ref[1, k, n] * x
        tc = twid_ref[k, :, 0:1]
        ts = twid_ref[k, :, 1:2]
        a = jnp.concatenate([re * tc + im * ts, im * tc - re * ts], axis=1)
        p = dot32(base_ref[0], base_ref[1], a)
        q = dot32(base_ref[2], base_ref[3], a)
        br = p[:, :both] + q[:, both:]
        bi = p[:, both:] - q[:, :both]
        sr, fr = br[:, :width], br[:, width:]
        si, fi = bi[:, :width], bi[:, width:]
        y = jnp.concatenate([sr * fr - si * fi, sr * fi + si * fr], axis=1)
        p = dot32(base_ref[0], base_ref[1], y)
        q = dot32(base_ref[2], base_ref[3], y)
        zr = p[:, :width] - q[:, width:]
        zi = p[:, width:] + q[:, :width]
        vr = zr * tc - zi * ts
        vi = zi * tc + zr * ts
        for n in range(blocks):
            acc_ref[n] += coef_ref[2, k, n] * vr - coef_ref[3, k, n] * vi
        return carry

    lax.fori_loop(0, blocks + 1, frequency, 0)

    back = []
    for j in range(1, blocks):
        d = (me + j) % blocks
        cs_send[j] = acc_ref[d].astype(jnp.bfloat16)
        copy = remote(cs_send.at[j], cs_recv.at[me], back_s.at[j], back_r.at[j], place(d))
        copy.start()
        back.append(copy)
    cs_recv[me] = acc_ref[me].astype(jnp.bfloat16)
    for copy in back:
        copy.wait_recv()
    for d in range(blocks):
        lanes = slice(d * width, (d + 1) * width)
        p = k_ref[:, lanes].astype(jnp.float32) * v_ref[:, lanes].astype(jnp.float32)
        conv = cs_recv[d].astype(jnp.float32)
        g_ref[core, :, lanes] = (
            q_ref[:, lanes].astype(jnp.float32) * (conv + skip_ref[:, lanes] * p)
        ).astype(jnp.bfloat16)
    swap = remote(g_ref.at[core], g_ref.at[core], g_s, g_r, sibling)
    swap.start()
    swap.wait()

    def weight_ready(c):
        source = c * per + core

        @pl.when(source != me)
        def _():
            remote(w_ref, w_all.at[c], w_s.at[0], w_r.at[c], sibling).wait_recv()

        @pl.when(source == me)
        def _():
            local.wait()

    def give(j):
        c = (z + j) % depth
        return remote(p_send.at[j], p_recv.at[j], p_s.at[j], p_r.at[j], {"ch": c})

    def project(j, carry):
        c = (z + j) % depth
        weight_ready(c)
        for half in range(2):
            part = jnp.dot(g_ref[half], w_all[c], preferred_element_type=jnp.float32)
            p_send[j, half] = part.astype(jnp.bfloat16)
        give(j).start()
        return carry

    lax.fori_loop(1, depth, project, 0)
    weight_ready(z)
    for half in range(2):
        p_own[half] = jnp.dot(g_ref[half], w_all[z], preferred_element_type=jnp.float32)
    for j in range(1, depth):
        give(j).wait_recv()

    def total(half):
        s = p_own[half]
        for j in range(1, depth):
            s += p_recv[j, half].astype(jnp.float32)
        return s.astype(jnp.bfloat16)

    o_send[...] = total(1 - core)
    last = remote(o_send, o_recv, o_s, o_r, sibling)
    last.start()
    out_ref[:, pl.ds(pl.multiple_of(core * cols, cols), cols)] = total(core)
    last.wait()
    out_ref[:, pl.ds(pl.multiple_of((1 - core) * cols, cols), cols)] = o_recv[...]

    for copy in entry + back:
        copy.wait_send()
    for dest, copy in weight:
        @pl.when(dest != me)
        def _():
            copy.wait_send()
    for j in range(1, depth):
        give(j).wait_send()


def fused(query_gate, key_proj, value_proj, filters, skip_gain, w_out):
    rows, channels = key_proj.shape
    cols = w_out.shape[1]
    blocks = lax.axis_size(SEQ)
    depth = lax.axis_size("ch")
    width = channels // blocks
    coef, base, twid = tables(blocks, rows)
    bf16, f32 = jnp.bfloat16, jnp.float32
    dma = pltpu.SemaphoreType.DMA
    return pl.pallas_call(
        layer_kernel,
        out_shape=jax.ShapeDtypeStruct((rows, channels), bf16),
        in_specs=[pl.BlockSpec(memory_space=pltpu.SMEM)] + [pl.BlockSpec(memory_space=pltpu.VMEM)] * 8,
        out_specs=pl.BlockSpec(memory_space=pltpu.VMEM),
        scratch_shapes=[
            pltpu.VMEM((blocks, rows, 2 * width), bf16),
            pltpu.VMEM((blocks, rows, 2 * width), bf16),
            pltpu.VMEM((blocks, rows, width), f32),
            pltpu.VMEM((blocks, rows, width), bf16),
            pltpu.VMEM((blocks, rows, width), bf16),
            pltpu.VMEM((2, rows, channels), bf16),
            pltpu.VMEM((depth,) + w_out.shape, bf16),
            pltpu.VMEM((depth, 2, rows, cols), bf16),
            pltpu.VMEM((depth, 2, rows, cols), bf16),
            pltpu.VMEM((2, rows, cols), f32),
            pltpu.VMEM((rows, cols), bf16),
            pltpu.VMEM((rows, cols), bf16),
            dma((blocks,)), dma((blocks,)), dma((blocks,)), dma((blocks,)),
            dma((blocks // 2,)), dma((depth,)),
            dma, dma, dma((depth,)), dma((depth,)), dma, dma, dma,
        ],
        compiler_params=pltpu.CompilerParams(
            collective_id=0, has_side_effects=True, vmem_limit_bytes=56 * 1024 * 1024
        ),
    )(jnp.asarray(coef), query_gate, key_proj, value_proj, filters, skip_gain[None, :], w_out,
      jnp.asarray(base), jnp.asarray(twid))


def shards(query_gate, key_proj, value_proj, filters, skip_gain, w_out):
    rows, channels = key_proj.shape
    seq = lax.axis_size(SEQ)
    width = channels // seq
    if width % 128 == 0 and seq == 2 * lax.axis_size("ch") and lax.axis_size("seqb") % 2 == 0:
        return fused(query_gate, key_proj, value_proj, filters, skip_gain, w_out)
    product = key_proj.astype(jnp.float32) * value_proj.astype(jnp.float32)
    pieces = lambda a: a.astype(jnp.bfloat16).reshape(rows, seq, width).transpose(1, 0, 2)
    stacked = jnp.concatenate([pieces(product), pieces(filters)], axis=2)
    columns = lax.all_to_all(stacked, SEQ, split_axis=0, concat_axis=0, tiled=True)
    spatial = lax.all_to_all(convolve(columns), SEQ, split_axis=0, concat_axis=0, tiled=True)
    convolved = spatial.transpose(1, 0, 2).reshape(rows, channels).astype(jnp.float32)
    gated_rows = (
        query_gate.astype(jnp.float32) * (convolved + skip_gain[None, :] * product)
    ).astype(jnp.bfloat16)
    weights = lax.all_gather(w_out, SEQ, axis=1, tiled=True)
    partial_sums = jnp.dot(gated_rows, weights, preferred_element_type=jnp.float32)
    return lax.psum_scatter(partial_sums, "ch", scatter_dimension=1, tiled=True).astype(
        jnp.bfloat16
    )


def solution(mesh):
    return jax.shard_map(
        shards,
        mesh=mesh,
        in_specs=(
            P(SEQ, "ch"),
            P(SEQ, "ch"),
            P(SEQ, "ch"),
            P(SEQ, "ch"),
            P("ch"),
            P("ch", SEQ),
        ),
        out_specs=P(SEQ, "ch"),
        check_vma=False,
    )
```

```python
import numpy as np

import jax
import jax.numpy as jnp
from jax import lax
from jax.experimental import pallas as pl
from jax.experimental.pallas import tpu as pltpu
from jax.sharding import PartitionSpec as P

SEQ = ("seqb", "seqt")


def split(x):
    hi = x.astype(jnp.bfloat16)
    return hi, (x - hi.astype(jnp.float32)).astype(jnp.bfloat16)


def dot32(m_hi, m_lo, a):
    a_hi, a_lo = split(a)
    dot = lambda p, q: jnp.dot(p, q, preferred_element_type=jnp.float32)
    return dot(m_hi, a_hi) + dot(m_lo, a_hi) + dot(m_hi, a_lo)


def conv_kernel(coef_ref, x_ref, base_ref, twid_ref, out_ref, acc_ref):
    blocks, rows, both = x_ref.shape
    width = both // 2
    k = pl.program_id(0)

    @pl.when(k == 0)
    def _():
        acc_ref[...] = jnp.zeros_like(acc_ref)

    re = jnp.zeros((rows, both), jnp.float32)
    im = jnp.zeros((rows, both), jnp.float32)
    for n in range(blocks):
        x = x_ref[n].astype(jnp.float32)
        re += coef_ref[0, k, n] * x
        im -= coef_ref[1, k, n] * x
    tc = twid_ref[0, :, 0:1]
    ts = twid_ref[0, :, 1:2]
    a = jnp.concatenate([re * tc + im * ts, im * tc - re * ts], axis=1)
    p = dot32(base_ref[0], base_ref[1], a)
    q = dot32(base_ref[2], base_ref[3], a)
    br = p[:, :both] + q[:, both:]
    bi = p[:, both:] - q[:, :both]
    sr, fr = br[:, :width], br[:, width:]
    si, fi = bi[:, :width], bi[:, width:]
    y = jnp.concatenate([sr * fr - si * fi, sr * fi + si * fr], axis=1)
    p = dot32(base_ref[0], base_ref[1], y)
    q = dot32(base_ref[2], base_ref[3], y)
    zr = p[:, :width] - q[:, width:]
    zi = p[:, width:] + q[:, :width]
    vr = zr * tc - zi * ts
    vi = zi * tc + zr * ts
    for n in range(blocks):
        acc_ref[n] += coef_ref[2, k, n] * vr - coef_ref[3, k, n] * vi

    @pl.when(k == blocks)
    def _():
        out_ref[...] = acc_ref[...].astype(out_ref.dtype)


def tables(blocks, rows):
    period = 2 * blocks * rows
    k = np.arange(blocks + 1)
    n = np.arange(blocks)
    ang = 2 * np.pi * ((k[:, None] * n[None, :]) % (2 * blocks)) / (2 * blocks)
    gain = np.where((k == 0) | (k == blocks), 1.0, 2.0)[:, None] / period
    coef = np.stack([np.cos(ang), np.sin(ang), gain * np.cos(ang), gain * np.sin(ang)])
    r = np.arange(rows)
    ang = 2 * np.pi * ((r[:, None] * r[None, :]) % rows) / rows
    parts = []
    for m in (np.cos(ang), np.sin(ang)):
        hi = m.astype(jnp.bfloat16)
        parts += [hi, (m - hi.astype(np.float64)).astype(jnp.bfloat16)]
    ang = 2 * np.pi * ((k[:, None] * r[None, :]) % period) / period
    twid = np.stack([np.cos(ang), np.sin(ang)], axis=-1)
    return coef.astype(np.float32), np.stack(parts), twid.astype(np.float32)


def convolve(columns):
    blocks, rows, both = columns.shape
    coef, base, twid = tables(blocks, rows)
    return pl.pallas_call(
        conv_kernel,
        grid=(blocks + 1,),
        out_shape=jax.ShapeDtypeStruct((blocks, rows, both // 2), jnp.bfloat16),
        in_specs=[
            pl.BlockSpec(memory_space=pltpu.SMEM),
            pl.BlockSpec((blocks, rows, both), lambda k: (0, 0, 0)),
            pl.BlockSpec((4, rows, rows), lambda k: (0, 0, 0)),
            pl.BlockSpec((1, rows, 2), lambda k: (k, 0, 0)),
        ],
        out_specs=pl.BlockSpec((blocks, rows, both // 2), lambda k: (0, 0, 0)),
        scratch_shapes=[pltpu.VMEM((blocks, rows, both // 2), jnp.float32)],
        compiler_params=pltpu.CompilerParams(vmem_limit_bytes=48 * 1024 * 1024),
        cost_estimate=pl.CostEstimate(
            flops=36 * (blocks + 1) * rows * rows * both, bytes_accessed=4 * 1024 * 1024, transcendentals=0
        ),
    )(jnp.asarray(coef), columns, jnp.asarray(base), jnp.asarray(twid))


MESH = pl.DeviceIdType.MESH


def layer_kernel(coef_ref, q_ref, k_ref, v_ref, f_ref, skip_ref, w_ref, base_ref, twid_ref, out_ref,
                 xs_send, xs_recv, acc_ref, cs_send, cs_recv, g_ref, w_all, p_send, p_recv, p_own,
                 o_send, o_recv, in_s, in_r, back_s, back_r, w_s, w_r, g_s, g_r, p_s, p_r, o_s, o_r, local_sem):
    seq_t = lax.axis_size("seqt")
    blocks = lax.axis_size("seqb") * seq_t
    depth = lax.axis_size("ch")
    ib, it, z = lax.axis_index("seqb"), lax.axis_index("seqt"), lax.axis_index("ch")
    me = ib * seq_t + it
    core = ib % 2
    rows, channels = k_ref.shape
    width = channels // blocks
    both = 2 * width
    cols = w_ref.shape[1]
    per = blocks // depth
    place = lambda s: {"seqb": s // seq_t, "seqt": s % seq_t}
    sibling = {"seqb": ib + 1 - 2 * core}

    def remote(src, dst, send, recv, where):
        return pltpu.make_async_remote_copy(
            src_ref=src, dst_ref=dst, send_sem=send, recv_sem=recv, device_id=where, device_id_type=MESH
        )

    barrier = pltpu.get_barrier_semaphore()
    for j in range(1, blocks):
        pl.semaphore_signal(barrier, inc=1, device_id=place((me + j) % blocks), device_id_type=MESH)
    for j in range(1, depth):
        pl.semaphore_signal(barrier, inc=1, device_id={"ch": (z + j) % depth}, device_id_type=MESH)

    def piece(d):
        lanes = pl.ds(pl.multiple_of(d * width, width), width)
        p = k_ref[:, lanes].astype(jnp.float32) * v_ref[:, lanes].astype(jnp.float32)
        return jnp.concatenate([p.astype(jnp.bfloat16), f_ref[:, lanes].astype(jnp.bfloat16)], axis=1)

    for j in range(1, blocks):
        xs_send[j] = piece((me + j) % blocks)
    pl.semaphore_wait(barrier, blocks + depth - 2)

    entry = [
        remote(xs_send.at[j], xs_recv.at[me], in_s.at[j], in_r.at[j], place((me + j) % blocks))
        for j in range(1, blocks)
    ]
    for copy in entry:
        copy.start()
    xs_recv[me] = piece(me)

    keep = me % per
    targets = [
        ((x * 2 + keep) * seq_t + t, x * seq_t + t)
        for x in range(blocks // seq_t // 2)
        for t in range(seq_t)
    ]
    weight = [
        (dest, remote(w_ref, w_all.at[me // per], w_s.at[i], w_r.at[me // per], place(dest)))
        for dest, i in targets
    ]
    local = pltpu.make_async_copy(w_ref, w_all.at[me // per], local_sem)
    mine = core == keep

    @pl.when(mine)
    def _():
        local.start()

    def start_weights(distant):
        for dest, copy in weight:
            near = ((dest // seq_t) // 2 == ib // 2) | (dest % seq_t == it)

            @pl.when(jnp.logical_not(near) if distant else near & (dest != me))
            def _():
                copy.start()

    start_weights(False)
    for copy in entry:
        copy.wait_recv()

    acc_ref[...] = jnp.zeros_like(acc_ref)

    def frequency(k, carry):
        re = jnp.zeros((rows, both), jnp.float32)
        im = jnp.zeros((rows, both), jnp.float32)
        for n in range(blocks):
            x = xs_recv[n].astype(jnp.float32)
            re += coef_ref[0, k, n] * x
            im -= coef_ref[1, k, n] * x
        tc = twid_ref[k, :, 0:1]
        ts = twid_ref[k, :, 1:2]
        a = jnp.concatenate([re * tc + im * ts, im * tc - re * ts], axis=1)
        p = dot32(base_ref[0], base_ref[1], a)
        q = dot32(base_ref[2], base_ref[3], a)
        br = p[:, :both] + q[:, both:]
        bi = p[:, both:] - q[:, :both]
        sr, fr = br[:, :width], br[:, width:]
        si, fi = bi[:, :width], bi[:, width:]
        y = jnp.concatenate([sr * fr - si * fi, sr * fi + si * fr], axis=1)
        p = dot32(base_ref[0], base_ref[1], y)
        q = dot32(base_ref[2], base_ref[3], y)
        zr = p[:, :width] - q[:, width:]
        zi = p[:, width:] + q[:, :width]
        vr = zr * tc - zi * ts
        vi = zi * tc + zr * ts
        for n in range(blocks):
            acc_ref[n] += coef_ref[2, k, n] * vr - coef_ref[3, k, n] * vi
        return carry

    lax.fori_loop(0, blocks + 1, frequency, 0)

    back = []
    for j in range(1, blocks):
        d = (me + j) % blocks
        cs_send[j] = acc_ref[d].astype(jnp.bfloat16)
        copy = remote(cs_send.at[j], cs_recv.at[me], back_s.at[j], back_r.at[j], place(d))
        copy.start()
        back.append(copy)
    start_weights(True)
    cs_recv[me] = acc_ref[me].astype(jnp.bfloat16)
    for copy in back:
        copy.wait_recv()
    for d in range(blocks):
        lanes = slice(d * width, (d + 1) * width)
        p = k_ref[:, lanes].astype(jnp.float32) * v_ref[:, lanes].astype(jnp.float32)
        conv = cs_recv[d].astype(jnp.float32)
        g_ref[core, :, lanes] = (
            q_ref[:, lanes].astype(jnp.float32) * (conv + skip_ref[:, lanes] * p)
        ).astype(jnp.bfloat16)
    swap = remote(g_ref.at[core], g_ref.at[core], g_s, g_r, sibling)
    swap.start()
    swap.wait()

    def weight_ready(c):
        source = c * per + core

        @pl.when(source != me)
        def _():
            remote(w_ref, w_all.at[c], w_s.at[0], w_r.at[c], sibling).wait_recv()

        @pl.when(source == me)
        def _():
            local.wait()

    def give(c):
        return remote(p_send.at[c], p_recv.at[z], p_s.at[c], p_r.at[z], {"ch": c})

    def take(c):
        return remote(p_send.at[c], p_recv.at[c], p_s.at[c], p_r.at[c], {"ch": c})

    def project(j, carry):
        c = (ib // 2 * 2 + j) % depth
        weight_ready(c)
        for half in range(2):
            part = jnp.dot(g_ref[half], w_all[c], preferred_element_type=jnp.float32)

            @pl.when(c == z)
            def _():
                p_own[half] = part

            @pl.when(c != z)
            def _():
                p_send[c, half] = part.astype(jnp.bfloat16)

        @pl.when(c != z)
        def _():
            give(c).start()

        return carry

    lax.fori_loop(0, depth, project, 0)
    for j in range(1, depth):
        take((z + j) % depth).wait_recv()

    def total(half):
        s = p_own[half]
        for j in range(1, depth):
            s += p_recv[(z + j) % depth, half].astype(jnp.float32)
        return s.astype(jnp.bfloat16)

    o_send[...] = total(1 - core)
    last = remote(o_send, o_recv, o_s, o_r, sibling)
    last.start()
    out_ref[:, pl.ds(pl.multiple_of(core * cols, cols), cols)] = total(core)
    last.wait()
    out_ref[:, pl.ds(pl.multiple_of((1 - core) * cols, cols), cols)] = o_recv[...]

    for copy in entry + back:
        copy.wait_send()
    for dest, copy in weight:
        @pl.when(dest != me)
        def _():
            copy.wait_send()
    for j in range(1, depth):
        give((z + j) % depth).wait_send()


def fused(query_gate, key_proj, value_proj, filters, skip_gain, w_out):
    rows, channels = key_proj.shape
    cols = w_out.shape[1]
    blocks = lax.axis_size(SEQ)
    depth = lax.axis_size("ch")
    width = channels // blocks
    coef, base, twid = tables(blocks, rows)
    bf16, f32 = jnp.bfloat16, jnp.float32
    dma = pltpu.SemaphoreType.DMA
    return pl.pallas_call(
        layer_kernel,
        out_shape=jax.ShapeDtypeStruct((rows, channels), bf16),
        in_specs=[pl.BlockSpec(memory_space=pltpu.SMEM)] + [pl.BlockSpec(memory_space=pltpu.VMEM)] * 8,
        out_specs=pl.BlockSpec(memory_space=pltpu.VMEM),
        scratch_shapes=[
            pltpu.VMEM((blocks, rows, 2 * width), bf16),
            pltpu.VMEM((blocks, rows, 2 * width), bf16),
            pltpu.VMEM((blocks, rows, width), f32),
            pltpu.VMEM((blocks, rows, width), bf16),
            pltpu.VMEM((blocks, rows, width), bf16),
            pltpu.VMEM((2, rows, channels), bf16),
            pltpu.VMEM((depth,) + w_out.shape, bf16),
            pltpu.VMEM((depth, 2, rows, cols), bf16),
            pltpu.VMEM((depth, 2, rows, cols), bf16),
            pltpu.VMEM((2, rows, cols), f32),
            pltpu.VMEM((rows, cols), bf16),
            pltpu.VMEM((rows, cols), bf16),
            dma((blocks,)), dma((blocks,)), dma((blocks,)), dma((blocks,)),
            dma((blocks // 2,)), dma((depth,)),
            dma, dma, dma((depth,)), dma((depth,)), dma, dma, dma,
        ],
        compiler_params=pltpu.CompilerParams(
            collective_id=0, has_side_effects=True, vmem_limit_bytes=56 * 1024 * 1024
        ),
    )(jnp.asarray(coef), query_gate, key_proj, value_proj, filters, skip_gain[None, :], w_out,
      jnp.asarray(base), jnp.asarray(twid))


def shards(query_gate, key_proj, value_proj, filters, skip_gain, w_out):
    rows, channels = key_proj.shape
    seq = lax.axis_size(SEQ)
    width = channels // seq
    if width % 128 == 0 and seq == 2 * lax.axis_size("ch") and lax.axis_size("seqb") % 2 == 0:
        return fused(query_gate, key_proj, value_proj, filters, skip_gain, w_out)
    product = key_proj.astype(jnp.float32) * value_proj.astype(jnp.float32)
    pieces = lambda a: a.astype(jnp.bfloat16).reshape(rows, seq, width).transpose(1, 0, 2)
    stacked = jnp.concatenate([pieces(product), pieces(filters)], axis=2)
    columns = lax.all_to_all(stacked, SEQ, split_axis=0, concat_axis=0, tiled=True)
    spatial = lax.all_to_all(convolve(columns), SEQ, split_axis=0, concat_axis=0, tiled=True)
    convolved = spatial.transpose(1, 0, 2).reshape(rows, channels).astype(jnp.float32)
    gated_rows = (
        query_gate.astype(jnp.float32) * (convolved + skip_gain[None, :] * product)
    ).astype(jnp.bfloat16)
    weights = lax.all_gather(w_out, SEQ, axis=1, tiled=True)
    partial_sums = jnp.dot(gated_rows, weights, preferred_element_type=jnp.float32)
    return lax.psum_scatter(partial_sums, "ch", scatter_dimension=1, tiled=True).astype(
        jnp.bfloat16
    )


def solution(mesh):
    return jax.shard_map(
        shards,
        mesh=mesh,
        in_specs=(
            P(SEQ, "ch"),
            P(SEQ, "ch"),
            P(SEQ, "ch"),
            P(SEQ, "ch"),
            P("ch"),
            P("ch", SEQ),
        ),
        out_specs=P(SEQ, "ch"),
        check_vma=False,
    )
```

```python
import numpy as np

import jax
import jax.numpy as jnp
from jax import lax
from jax.experimental import pallas as pl
from jax.experimental.pallas import tpu as pltpu
from jax.sharding import PartitionSpec as P

SEQ = ("seqb", "seqt")


def split(x):
    hi = x.astype(jnp.bfloat16)
    return hi, (x - hi.astype(jnp.float32)).astype(jnp.bfloat16)


def dot32(m_hi, m_lo, a):
    a_hi, a_lo = split(a)
    dot = lambda p, q: jnp.dot(p, q, preferred_element_type=jnp.float32)
    return dot(m_hi, a_hi) + dot(m_lo, a_hi) + dot(m_hi, a_lo)


def conv_kernel(coef_ref, x_ref, base_ref, twid_ref, out_ref, acc_ref):
    blocks, rows, both = x_ref.shape
    width = both // 2
    k = pl.program_id(0)

    @pl.when(k == 0)
    def _():
        acc_ref[...] = jnp.zeros_like(acc_ref)

    re = jnp.zeros((rows, both), jnp.float32)
    im = jnp.zeros((rows, both), jnp.float32)
    for n in range(blocks):
        x = x_ref[n].astype(jnp.float32)
        re += coef_ref[0, k, n] * x
        im -= coef_ref[1, k, n] * x
    tc = twid_ref[0, :, 0:1]
    ts = twid_ref[0, :, 1:2]
    a = jnp.concatenate([re * tc + im * ts, im * tc - re * ts], axis=1)
    p = dot32(base_ref[0], base_ref[1], a)
    q = dot32(base_ref[2], base_ref[3], a)
    br = p[:, :both] + q[:, both:]
    bi = p[:, both:] - q[:, :both]
    sr, fr = br[:, :width], br[:, width:]
    si, fi = bi[:, :width], bi[:, width:]
    y = jnp.concatenate([sr * fr - si * fi, sr * fi + si * fr], axis=1)
    p = dot32(base_ref[0], base_ref[1], y)
    q = dot32(base_ref[2], base_ref[3], y)
    zr = p[:, :width] - q[:, width:]
    zi = p[:, width:] + q[:, :width]
    vr = zr * tc - zi * ts
    vi = zi * tc + zr * ts
    for n in range(blocks):
        acc_ref[n] += coef_ref[2, k, n] * vr - coef_ref[3, k, n] * vi

    @pl.when(k == blocks)
    def _():
        out_ref[...] = acc_ref[...].astype(out_ref.dtype)


def tables(blocks, rows):
    period = 2 * blocks * rows
    k = np.arange(blocks + 1)
    n = np.arange(blocks)
    ang = 2 * np.pi * ((k[:, None] * n[None, :]) % (2 * blocks)) / (2 * blocks)
    gain = np.where((k == 0) | (k == blocks), 1.0, 2.0)[:, None] / period
    coef = np.stack([np.cos(ang), np.sin(ang), gain * np.cos(ang), gain * np.sin(ang)])
    r = np.arange(rows)
    ang = 2 * np.pi * ((r[:, None] * r[None, :]) % rows) / rows
    parts = []
    for m in (np.cos(ang), np.sin(ang)):
        hi = m.astype(jnp.bfloat16)
        parts += [hi, (m - hi.astype(np.float64)).astype(jnp.bfloat16)]
    ang = 2 * np.pi * ((k[:, None] * r[None, :]) % period) / period
    twid = np.stack([np.cos(ang), np.sin(ang)], axis=-1)
    return coef.astype(np.float32), np.stack(parts), twid.astype(np.float32)


def convolve(columns):
    blocks, rows, both = columns.shape
    coef, base, twid = tables(blocks, rows)
    return pl.pallas_call(
        conv_kernel,
        grid=(blocks + 1,),
        out_shape=jax.ShapeDtypeStruct((blocks, rows, both // 2), jnp.bfloat16),
        in_specs=[
            pl.BlockSpec(memory_space=pltpu.SMEM),
            pl.BlockSpec((blocks, rows, both), lambda k: (0, 0, 0)),
            pl.BlockSpec((4, rows, rows), lambda k: (0, 0, 0)),
            pl.BlockSpec((1, rows, 2), lambda k: (k, 0, 0)),
        ],
        out_specs=pl.BlockSpec((blocks, rows, both // 2), lambda k: (0, 0, 0)),
        scratch_shapes=[pltpu.VMEM((blocks, rows, both // 2), jnp.float32)],
        compiler_params=pltpu.CompilerParams(vmem_limit_bytes=48 * 1024 * 1024),
        cost_estimate=pl.CostEstimate(
            flops=36 * (blocks + 1) * rows * rows * both, bytes_accessed=4 * 1024 * 1024, transcendentals=0
        ),
    )(jnp.asarray(coef), columns, jnp.asarray(base), jnp.asarray(twid))


MESH = pl.DeviceIdType.MESH


def layer_kernel(coef_ref, q_ref, k_ref, v_ref, f_ref, skip_ref, w_ref, base_ref, twid_ref, out_ref,
                 xs_send, xs_recv, acc_ref, cs_send, cs_recv, g_ref, w_all, p_send, p_recv, p_own,
                 o_send, o_recv, in_s, in_r, back_s, back_r, w_s, w_r, g_s, g_r, p_s, p_r, o_s, o_r, local_sem, f_s, r_recv, p_far, r_r):
    seq_t = lax.axis_size("seqt")
    blocks = lax.axis_size("seqb") * seq_t
    depth = lax.axis_size("ch")
    ib, it, z = lax.axis_index("seqb"), lax.axis_index("seqt"), lax.axis_index("ch")
    me = ib * seq_t + it
    core = ib % 2
    rows, channels = k_ref.shape
    width = channels // blocks
    both = 2 * width
    cols = w_ref.shape[1]
    per = blocks // depth
    place = lambda s: {"seqb": s // seq_t, "seqt": s % seq_t}
    sibling = {"seqb": ib + 1 - 2 * core}

    def remote(src, dst, send, recv, where):
        return pltpu.make_async_remote_copy(
            src_ref=src, dst_ref=dst, send_sem=send, recv_sem=recv, device_id=where, device_id_type=MESH
        )

    barrier = pltpu.get_barrier_semaphore()
    for j in range(1, blocks):
        pl.semaphore_signal(barrier, inc=1, device_id=place((me + j) % blocks), device_id_type=MESH)
    for j in range(1, depth):
        pl.semaphore_signal(barrier, inc=1, device_id={"ch": (z + j) % depth}, device_id_type=MESH)

    def piece(d):
        lanes = pl.ds(pl.multiple_of(d * width, width), width)
        p = k_ref[:, lanes].astype(jnp.float32) * v_ref[:, lanes].astype(jnp.float32)
        return jnp.concatenate([p.astype(jnp.bfloat16), f_ref[:, lanes].astype(jnp.bfloat16)], axis=1)

    for j in range(1, blocks):
        xs_send[j] = piece((me + j) % blocks)
    pl.semaphore_wait(barrier, blocks + depth - 2)

    entry = [
        remote(xs_send.at[j], xs_recv.at[me], in_s.at[j], in_r.at[j], place((me + j) % blocks))
        for j in range(1, blocks)
    ]
    for copy in entry:
        copy.start()
    xs_recv[me] = piece(me)

    keep = me % per
    targets = [
        ((x * 2 + keep) * seq_t + t, x * seq_t + t)
        for x in range(blocks // seq_t // 2)
        for t in range(seq_t)
    ]
    weight = [
        (dest, remote(w_ref, w_all.at[me // per], w_s.at[i], w_r.at[me // per], place(dest)))
        for dest, i in targets
    ]
    local = pltpu.make_async_copy(w_ref, w_all.at[me // per], local_sem)
    mine = core == keep

    @pl.when(mine)
    def _():
        local.start()

    def start_weights():
        for dest, copy in weight:
            near = ((dest // seq_t) // 2 == ib // 2) | (dest % seq_t == it)

            @pl.when(near & (dest != me))
            def _():
                copy.start()

    start_weights()
    for copy in entry:
        copy.wait_recv()

    acc_ref[...] = jnp.zeros_like(acc_ref)

    def frequency(k, carry):
        re = jnp.zeros((rows, both), jnp.float32)
        im = jnp.zeros((rows, both), jnp.float32)
        for n in range(blocks):
            x = xs_recv[n].astype(jnp.float32)
            re += coef_ref[0, k, n] * x
            im -= coef_ref[1, k, n] * x
        tc = twid_ref[k, :, 0:1]
        ts = twid_ref[k, :, 1:2]
        a = jnp.concatenate([re * tc + im * ts, im * tc - re * ts], axis=1)
        p = dot32(base_ref[0], base_ref[1], a)
        q = dot32(base_ref[2], base_ref[3], a)
        br = p[:, :both] + q[:, both:]
        bi = p[:, both:] - q[:, :both]
        sr, fr = br[:, :width], br[:, width:]
        si, fi = bi[:, :width], bi[:, width:]
        y = jnp.concatenate([sr * fr - si * fi, sr * fi + si * fr], axis=1)
        p = dot32(base_ref[0], base_ref[1], y)
        q = dot32(base_ref[2], base_ref[3], y)
        zr = p[:, :width] - q[:, width:]
        zi = p[:, width:] + q[:, :width]
        vr = zr * tc - zi * ts
        vi = zi * tc + zr * ts
        for n in range(blocks):
            acc_ref[n] += coef_ref[2, k, n] * vr - coef_ref[3, k, n] * vi
        return carry

    lax.fori_loop(0, blocks + 1, frequency, 0)

    back = []
    for j in range(1, blocks):
        d = (me + j) % blocks
        cs_send[j] = acc_ref[d].astype(jnp.bfloat16)
        copy = remote(cs_send.at[j], cs_recv.at[me], back_s.at[j], back_r.at[j], place(d))
        copy.start()
        back.append(copy)
    same = it == core
    passed = jnp.where(same, (1 - ib // 2) * 2, ib // 2 * 2 + 1)
    onward = {"seqb": jnp.where(same, ib, (ib + 2) % 4), "seqt": jnp.where(same, 1 - it, it)}
    forward = remote(w_all.at[passed], w_all.at[passed], f_s, w_r.at[passed], onward)
    forward.wait_recv()
    forward.start()
    cs_recv[me] = acc_ref[me].astype(jnp.bfloat16)
    for copy in back:
        copy.wait_recv()
    for d in range(blocks):
        lanes = slice(d * width, (d + 1) * width)
        p = k_ref[:, lanes].astype(jnp.float32) * v_ref[:, lanes].astype(jnp.float32)
        conv = cs_recv[d].astype(jnp.float32)
        g_ref[core, :, lanes] = (
            q_ref[:, lanes].astype(jnp.float32) * (conv + skip_ref[:, lanes] * p)
        ).astype(jnp.bfloat16)
    swap = remote(g_ref.at[core], g_ref.at[core], g_s, g_r, sibling)
    swap.start()
    swap.wait()

    def weight_ready(c):
        source = c * per + core

        @pl.when((source != me) & (c != passed))
        def _():
            remote(w_ref, w_all.at[c], w_s.at[0], w_r.at[c], sibling).wait_recv()

        @pl.when(source == me)
        def _():
            local.wait()

    def give(c):
        return remote(p_send.at[c], p_recv.at[z], p_s.at[c], p_r.at[z], {"ch": c})

    def take(c):
        return remote(p_send.at[c], p_recv.at[c], p_s.at[c], p_r.at[c], {"ch": c})

    beside = z + 1 - 2 * (z % 2)
    outer = (z == 0) | (z == 3)
    inner = jnp.logical_not(outer)
    far = [jnp.where(z < 2, 3 - i, i) for i in range(2)]
    relay = [
        remote(p_send.at[far[i]], r_recv.at[i], p_s.at[far[i]], r_r.at[i], {"ch": beside})
        for i in range(2)
    ]

    def partial(c, half):
        return jnp.dot(g_ref[half], w_all[c], preferred_element_type=jnp.float32)

    for i in range(2):
        weight_ready(far[i])
        for half in range(2):
            part = partial(far[i], half)

            @pl.when(outer)
            def _():
                p_send[far[i], half] = part.astype(jnp.bfloat16)

            @pl.when(inner)
            def _():
                p_far[i, half] = part

        @pl.when(outer)
        def _():
            if i:
                relay[0].wait_send()
            relay[i].start()

    weight_ready(beside)
    for half in range(2):
        p_send[beside, half] = partial(beside, half).astype(jnp.bfloat16)

    @pl.when(inner)
    def _():
        give(beside).start()

    weight_ready(z)
    for half in range(2):
        p_own[half] = partial(z, half)

    @pl.when(outer)
    def _():
        relay[1].wait_send()
        give(beside).start()

    @pl.when(inner)
    def _():
        for i in range(2):
            relay[i].wait_recv()
            for half in range(2):
                p_send[far[i], half] = (
                    p_far[i, half] + r_recv[i, half].astype(jnp.float32)
                ).astype(jnp.bfloat16)
            give(far[i]).start()

    across = jnp.where(z < 2, 2, 1)
    take(across).wait_recv()
    take(beside).wait_recv()

    def total(half):
        s = p_own[half] + p_recv[beside, half].astype(jnp.float32)
        return (s + p_recv[across, half].astype(jnp.float32)).astype(jnp.bfloat16)

    o_send[...] = total(1 - core)
    last = remote(o_send, o_recv, o_s, o_r, sibling)
    last.start()
    out_ref[:, pl.ds(pl.multiple_of(core * cols, cols), cols)] = total(core)
    last.wait()
    out_ref[:, pl.ds(pl.multiple_of((1 - core) * cols, cols), cols)] = o_recv[...]

    for copy in entry + back:
        copy.wait_send()
    for dest, copy in weight:
        near = ((dest // seq_t) // 2 == ib // 2) | (dest % seq_t == it)

        @pl.when(near & (dest != me))
        def _():
            copy.wait_send()
    forward.wait_send()
    give(beside).wait_send()

    @pl.when(inner)
    def _():
        for i in range(2):
            give(far[i]).wait_send()


def fused(query_gate, key_proj, value_proj, filters, skip_gain, w_out):
    rows, channels = key_proj.shape
    cols = w_out.shape[1]
    blocks = lax.axis_size(SEQ)
    depth = lax.axis_size("ch")
    width = channels // blocks
    coef, base, twid = tables(blocks, rows)
    bf16, f32 = jnp.bfloat16, jnp.float32
    dma = pltpu.SemaphoreType.DMA
    return pl.pallas_call(
        layer_kernel,
        out_shape=jax.ShapeDtypeStruct((rows, channels), bf16),
        in_specs=[pl.BlockSpec(memory_space=pltpu.SMEM)] + [pl.BlockSpec(memory_space=pltpu.VMEM)] * 8,
        out_specs=pl.BlockSpec(memory_space=pltpu.VMEM),
        scratch_shapes=[
            pltpu.VMEM((blocks, rows, 2 * width), bf16),
            pltpu.VMEM((blocks, rows, 2 * width), bf16),
            pltpu.VMEM((blocks, rows, width), f32),
            pltpu.VMEM((blocks, rows, width), bf16),
            pltpu.VMEM((blocks, rows, width), bf16),
            pltpu.VMEM((2, rows, channels), bf16),
            pltpu.VMEM((depth,) + w_out.shape, bf16),
            pltpu.VMEM((depth, 2, rows, cols), bf16),
            pltpu.VMEM((depth, 2, rows, cols), bf16),
            pltpu.VMEM((2, rows, cols), f32),
            pltpu.VMEM((rows, cols), bf16),
            pltpu.VMEM((rows, cols), bf16),
            dma((blocks,)), dma((blocks,)), dma((blocks,)), dma((blocks,)),
            dma((blocks // 2,)), dma((depth,)),
            dma, dma, dma((depth,)), dma((depth,)), dma, dma, dma, dma,
            pltpu.VMEM((2, 2, rows, cols), bf16), pltpu.VMEM((2, 2, rows, cols), f32), dma((2,)),
        ],
        compiler_params=pltpu.CompilerParams(
            collective_id=0, has_side_effects=True, vmem_limit_bytes=56 * 1024 * 1024
        ),
    )(jnp.asarray(coef), query_gate, key_proj, value_proj, filters, skip_gain[None, :], w_out,
      jnp.asarray(base), jnp.asarray(twid))


def shards(query_gate, key_proj, value_proj, filters, skip_gain, w_out):
    rows, channels = key_proj.shape
    seq = lax.axis_size(SEQ)
    width = channels // seq
    if width % 128 == 0 and seq == 2 * lax.axis_size("ch") and lax.axis_size("seqb") == 4 and lax.axis_size("ch") == 4:
        return fused(query_gate, key_proj, value_proj, filters, skip_gain, w_out)
    product = key_proj.astype(jnp.float32) * value_proj.astype(jnp.float32)
    pieces = lambda a: a.astype(jnp.bfloat16).reshape(rows, seq, width).transpose(1, 0, 2)
    stacked = jnp.concatenate([pieces(product), pieces(filters)], axis=2)
    columns = lax.all_to_all(stacked, SEQ, split_axis=0, concat_axis=0, tiled=True)
    spatial = lax.all_to_all(convolve(columns), SEQ, split_axis=0, concat_axis=0, tiled=True)
    convolved = spatial.transpose(1, 0, 2).reshape(rows, channels).astype(jnp.float32)
    gated_rows = (
        query_gate.astype(jnp.float32) * (convolved + skip_gain[None, :] * product)
    ).astype(jnp.bfloat16)
    weights = lax.all_gather(w_out, SEQ, axis=1, tiled=True)
    partial_sums = jnp.dot(gated_rows, weights, preferred_element_type=jnp.float32)
    return lax.psum_scatter(partial_sums, "ch", scatter_dimension=1, tiled=True).astype(
        jnp.bfloat16
    )


def solution(mesh):
    return jax.shard_map(
        shards,
        mesh=mesh,
        in_specs=(
            P(SEQ, "ch"),
            P(SEQ, "ch"),
            P(SEQ, "ch"),
            P(SEQ, "ch"),
            P("ch"),
            P("ch", SEQ),
        ),
        out_specs=P(SEQ, "ch"),
        check_vma=False,
    )
```
